256 devices in a mesh: walker: 16 (over x, y), tangent: 8 (over z), feat: 2 (over core).
Axes of the slice: x: 4, y: 4, z: 8, core: 2. Of those that a mesh axis runs over, the one named last changes fastest.
Arguments:
- value_in: bfloat16 [512, 512], P('walker', 'feat'), may hold values from -0.94921875 to 0.94921875
- tang_in: bfloat16 [512, 768, 512], P('walker', 'tangent', 'feat'), may hold values from -1.01 to 1.01
- lap_in: bfloat16 [512, 512], P('walker', 'feat'), may hold values from -6 to 6
- w_first: bfloat16 [512, 512], P(('walker', 'tangent', 'feat')), may hold values from -0.25 to 0.25
- b_first: float32 [512], replicated, may hold values from -3 to 3
- w_second: bfloat16 [512, 512], P(('walker', 'tangent', 'feat')), may hold values from -0.25 to 0.25
- b_second: float32 [512], replicated, may hold values from -3 to 3
- readout: float32 [512], replicated, may hold values from -0.6 to 0.6
Outputs:
- log_amplitude: float32 [512], P('walker')
- gradient: float32 [512, 768], P('walker', 'tangent')
- kinetic: float32 [512], P('walker')
The draws below stay inside these ranges and needn't reach their ends.
All inputs are finite; a program needn't handle non-finite values.
Results may differ from the reference program's by a relative error of at most 0.0044.
Values may be sent and summed in bfloat16 or wider, within the bound.
No kernel may reach another device: no remote copies, remote signals or barrier semaphores. Data moves between devices by JAX's collectives and lax.ppermute only.
A program may use at most 64 MiB of HBM per device.

```python
import math
import jax
import jax.numpy as jnp
from jax import lax

D = 512
W_DEV = 32
TANGENTS = 768
WALKERS = 512


def draw_tang_in(key, part):
    first_key, second_key = jax.random.split(key, 2)
    columns = jnp.arange(TANGENTS, dtype=jnp.float32)
    growth = jnp.exp(math.log(3.0) * columns / (TANGENTS - 1))[None, :, None]
    spread = jax.random.uniform(second_key, (WALKERS, TANGENTS, 1), minval=0.6, maxval=1.4)
    pattern = jnp.clip(jax.random.normal(first_key, (WALKERS, TANGENTS, D)), -6.0, 6.0)
    return (0.04 * growth * spread * pattern).astype(jnp.bfloat16)


def steps_of(key, extent, cuts, low, top_value):
    def one(position, shards_of):
        draws = jax.random.uniform(jax.random.fold_in(jax.random.fold_in(key, 6), position), (shards_of,), jnp.float32, low / len(cuts), top_value / len(cuts))
        return jnp.repeat(jnp.exp(draws), extent[position] // shards_of).reshape((-1,) + (1,) * (len(extent) - position - 1))

    level = one(*cuts[0])
    for cut in cuts[1:]:
        level = level * one(*cut)
    return level


def normal_values(own_key, shape, scale, most, cuts=(), held_as=jnp.bfloat16):
    loudness = steps_of(own_key, shape, cuts, -0.22, 0.18) if cuts else 1.0
    result = jax.random.normal(own_key, shape, jnp.float32) * scale * loudness
    return jnp.minimum(jnp.maximum(result, -most), most).astype(held_as)


def setup_inputs(seed: int = 0) -> dict:
    arg_keys = jax.random.split(jax.random.key(seed), 9)
    return {
        "value_in": jnp.clip(jax.random.uniform(arg_keys[0], (WALKERS, D), jnp.float32, -0.94921875, 0.94921875) * steps_of(arg_keys[0], (WALKERS, D), ((0, 16), (1, 2)), -0.4, 0.0), -0.94921875, 0.94921875).astype(jnp.bfloat16),
        "tang_in": draw_tang_in(jax.random.fold_in(arg_keys[8], 71), 0),
        "lap_in": normal_values(arg_keys[2], (WALKERS, D), 1.0, 6.0, ((0, 16), (1, 2))),
        "w_first": normal_values(arg_keys[3], (D, D), D ** -0.5, 0.25, ((0, 256),)),
        "b_first": normal_values(arg_keys[4], (D,), 0.5, 3.0, (), jnp.float32),
        "w_second": normal_values(arg_keys[5], (D, D), D ** -0.5, 0.25, ((0, 256),)),
        "b_second": normal_values(arg_keys[6], (D,), 0.5, 3.0, (), jnp.float32),
        "readout": normal_values(arg_keys[7], (D,), 0.1, 0.6, (), jnp.float32),
    }


def tanh_layer(value, tangents, laplacian, weight, bias):
    pre_act = jnp.dot(value, weight, preferred_element_type=jnp.float32) + bias
    lap_pre = jnp.dot(laplacian, weight, preferred_element_type=jnp.float32)
    count_w, count_t, width = tangents.shape
    grad_pre = jnp.dot(tangents.reshape(count_w * count_t, width), weight, preferred_element_type=jnp.float32)
    grad_pre = grad_pre.reshape(count_w, count_t, weight.shape[1])
    hidden = jnp.tanh(pre_act)
    slope = 1.0 - hidden * hidden
    bend = -2.0 * hidden * slope
    curvature = jnp.sum(grad_pre * grad_pre, axis=1)
    return hidden, slope, bend, grad_pre, lap_pre, curvature


def reference(value_in, tang_in, lap_in, w_first, b_first, w_second, b_second, readout):
    blocks = WALKERS // W_DEV

    def one_block(inputs):
        value, tangents, laplacian = inputs
        hidden, slope, bend, grad_pre, lap_pre, curvature = tanh_layer(value, tangents, laplacian, w_first, b_first)
        value_two = hidden.astype(jnp.bfloat16)
        tang_two = (slope[:, None, :] * grad_pre).astype(jnp.bfloat16)
        lap_two = (slope * lap_pre + bend * curvature).astype(jnp.bfloat16)
        hidden, slope, bend, grad_pre, lap_pre, curvature = tanh_layer(value_two, tang_two, lap_two, w_second, b_second)
        log_amplitude = jnp.sum(readout * hidden, axis=-1)
        gradient = jnp.sum(grad_pre * (readout * slope)[:, None, :], axis=-1)
        laplace = jnp.sum(readout * (slope * lap_pre + bend * curvature), axis=-1)
        kinetic = -0.5 * (laplace + jnp.sum(gradient * gradient, axis=-1))
        return log_amplitude, gradient, kinetic

    log_amplitude, gradient, kinetic = lax.map(one_block, (value_in.reshape(blocks, W_DEV, D), tang_in.reshape(blocks, W_DEV, TANGENTS, D), lap_in.reshape(blocks, W_DEV, D)))
    return log_amplitude.reshape(WALKERS), gradient.reshape(WALKERS, TANGENTS), kinetic.reshape(WALKERS)
```

```python
import functools

import jax
import jax.numpy as jnp
from jax import lax
from jax.experimental import pallas as pl
from jax.experimental.pallas import tpu as pltpu
from jax.sharding import PartitionSpec as P

BF16, F32 = jnp.bfloat16, jnp.float32


def layer_kernel(cfg, scal, t_own, t_oth, v_own, v_oth, l_own, l_oth, w_own, w_oth, b1, b2, rd,
                 amp_out, grad_out, s_out, s1_sc, s2_sc, c1_sc, c2_sc):
    half, mine, group, per_core = cfg
    c = scal[0]
    first_z = scal[1] == 0
    weights = (w_own, w_oth)
    k_half = (c, 1 - c)
    blocks = w_own.shape[0] // 2
    rows = w_own.shape[1] // 2

    def wblk(layer, k, j):
        w = weights[j][pl.ds(k_half[k] * blocks, blocks), layer * rows:(layer + 1) * rows, :]
        return w.reshape(half, half)

    def vec(ref, j):
        return ref[:, pl.ds(pl.multiple_of(k_half[j] * half, half), half)]

    def mm(a, b):
        return jnp.dot(a, b, preferred_element_type=F32)

    def layer_mm(xs, layer, j):
        return mm(xs[0], wblk(layer, 0, j)) + mm(xs[1], wblk(layer, 1, j))

    base = c * mine
    v = (v_own[...], v_oth[...])
    hid1 = [jnp.tanh(layer_mm(v, 0, j) + vec(b1, j)) for j in (0, 1)]
    hid1_b = [h.astype(BF16) for h in hid1]
    hid2 = [jnp.tanh(layer_mm(hid1_b, 1, j) + vec(b2, j)) for j in (0, 1)]
    amp_out[...] = sum(jnp.sum(vec(rd, j) * hid2[j], axis=-1, keepdims=True) for j in (0, 1))
    for j in (0, 1):
        s1_sc[:, j * half:(j + 1) * half] = hid1[j]
        s2_sc[:, j * half:(j + 1) * half] = hid2[j]
    per = t_own.shape[1]
    h1m = s1_sc[pl.ds(base, mine), :]
    h2m = s2_sc[pl.ds(base, mine), :]
    slope1 = 1.0 - h1m * h1m
    slope2 = 1.0 - h2m * h2m
    rdv = jnp.concatenate([vec(rd, 0), vec(rd, 1)], axis=1)
    rs = rdv * slope2
    for g in range(mine // group):
        lo, hi = g * group, (g + 1) * group
        ts = [t[pl.ds(base + lo, group)].reshape(group * per, half) for t in (t_own, t_oth)]
        t2 = []
        for j in (0, 1):
            cols = slice(j * half, (j + 1) * half)
            g1 = layer_mm(ts, 0, j).reshape(group, per, half)
            c1_sc[lo:hi, cols] = jnp.sum(g1 * g1, axis=1)
            t2.append((g1 * slope1[lo:hi, None, cols]).astype(BF16).reshape(group * per, half))
        prod = None
        for j in (0, 1):
            cols = slice(j * half, (j + 1) * half)
            g2 = layer_mm(t2, 1, j).reshape(group, per, half)
            c2_sc[lo:hi, cols] = jnp.sum(g2 * g2, axis=1)
            term = g2 * rs[lo:hi, None, cols]
            prod = term if prod is None else prod + term
        grad_out[lo:hi, :] = jnp.sum(prod, axis=-1)
    lap = (l_own[pl.ds(base, mine), :], l_oth[pl.ds(base, mine), :])
    lap_two = []
    for j in (0, 1):
        cols = slice(j * half, (j + 1) * half)
        s1, h1 = slope1[:, cols], h1m[:, cols]
        direct = jnp.where(first_z, s1 * layer_mm(lap, 0, j), 0.0)
        lap_two.append(direct + (-2.0 * h1 * s1) * c1_sc[:, cols])
    high = [x.astype(BF16) for x in lap_two]
    low = [(x - h.astype(F32)).astype(BF16) for x, h in zip(lap_two, high)]
    total = jnp.zeros((mine, 1), F32)
    for j in (0, 1):
        cols = slice(j * half, (j + 1) * half)
        lapin2 = layer_mm(high, 1, j) + layer_mm(low, 1, j)
        s2, h2 = slope2[:, cols], h2m[:, cols]
        inner = s2 * lapin2 + (-2.0 * h2 * s2) * c2_sc[:, cols]
        total += jnp.sum(vec(rd, j) * inner, axis=-1, keepdims=True)
    gr = grad_out[...]
    total += jnp.sum(gr * gr, axis=-1, keepdims=True)
    s_out[...] = total


def per_device(value_in, tang_in, lap_in, w_first, b_first, w_second, b_second, readout):
    walkers, half = value_in.shape
    per = tang_in.shape[1]
    n_z, n_c, n_w = lax.axis_size("tangent"), lax.axis_size("feat"), lax.axis_size("walker")
    mine = walkers // n_c
    swap = [(0, 1), (1, 0)]
    c = lax.axis_index("feat")
    z = lax.axis_index("tangent")

    t_oth = lax.ppermute(tang_in, "feat", swap)
    v_oth = lax.ppermute(value_in, "feat", swap)
    l_oth = lax.ppermute(lap_in, "feat", swap)

    rows = w_first.shape[0]
    pair = jnp.concatenate([w_first, w_second], axis=0).reshape(2 * rows, n_c, half)
    piece = jnp.transpose(pair, (1, 0, 2))
    sent = jnp.broadcast_to(piece[None], (n_z, n_c, 2 * rows, half)).reshape(n_z * n_c, 2 * rows, half)
    got = lax.all_to_all(sent, ("tangent", "feat"), 0, 0, tiled=True)
    got = jnp.transpose(got.reshape(n_z * n_c, 2, rows, half), (1, 0, 2, 3)).reshape(-1, half)
    sent = jnp.broadcast_to(got[None], (n_w,) + got.shape)
    w_own = lax.all_to_all(sent, "walker", 0, 0, tiled=True)
    w_oth = lax.ppermute(w_own, "feat", swap)

    scal = jnp.stack([c, z]).astype(jnp.int32)
    group = 8
    vm = pl.BlockSpec(memory_space=pltpu.VMEM)
    amp, grad, part = pl.pallas_call(
        functools.partial(layer_kernel, (half, mine, group, mine)),
        out_shape=(
            jax.ShapeDtypeStruct((walkers, 1), F32),
            jax.ShapeDtypeStruct((mine, per), F32),
            jax.ShapeDtypeStruct((mine, 1), F32),
        ),
        in_specs=[pl.BlockSpec(memory_space=pltpu.SMEM)] + [vm] * 11,
        out_specs=(vm, vm, vm),
        scratch_shapes=[
            pltpu.VMEM((walkers, 2 * half), F32),
            pltpu.VMEM((walkers, 2 * half), F32),
            pltpu.VMEM((mine, 2 * half), F32),
            pltpu.VMEM((mine, 2 * half), F32),
        ],
        compiler_params=pltpu.CompilerParams(vmem_limit_bytes=40 * 1024 * 1024),
        name="layers",
    )(scal, tang_in, t_oth, value_in, v_oth, lap_in, l_oth, w_own, w_oth,
      b_first[None], b_second[None], readout[None])

    g_oth = lax.ppermute(grad, "feat", swap)
    row = jnp.pad(part.reshape(1, mine), ((0, 0), (0, 128 - mine)))
    sums = lax.all_to_all(jnp.broadcast_to(row[None], (n_z * n_c, 1, 128)), ("tangent", "feat"), 0, 0, tiled=True)
    squares = jnp.sum(sums.reshape(n_z, n_c, 128), axis=0)[:, :mine].reshape(walkers)
    first = jnp.where(c == 0, grad, g_oth)
    second = jnp.where(c == 0, g_oth, grad)
    return amp.reshape(walkers), jnp.concatenate([first, second], axis=0), -0.5 * squares


def solution(mesh):
    placed = (
        P("walker", "feat"),
        P("walker", "tangent", "feat"),
        P("walker", "feat"),
        P(("walker", "tangent", "feat"), None),
        P(),
        P(("walker", "tangent", "feat"), None),
        P(),
        P(),
    )
    return jax.shard_map(
        per_device,
        mesh=mesh,
        in_specs=placed,
        out_specs=(P("walker"), P("walker", "tangent"), P("walker")),
        check_vma=False,
    )
```

```python
import jax
import jax.numpy as jnp
from jax import lax
from jax.experimental import pallas as pl
from jax.experimental.pallas import tpu as pltpu
from jax.sharding import PartitionSpec as P

BF16, F32 = jnp.bfloat16, jnp.float32
GROUP = 8
LANES = 128


def mm(a, b):
    return jnp.dot(a, b, preferred_element_type=F32)


class Halves:
    def __init__(self, c, half, w_own, w_oth, layer):
        self.index = (c, 1 - c)
        self.half = half
        self.weights = (w_own, w_oth)
        self.blocks = w_own.shape[0] // 2
        rows = w_own.shape[1] // 2
        self.rows = slice(layer * rows, (layer + 1) * rows)

    def block(self, k, j):
        w = self.weights[j][pl.ds(self.index[k] * self.blocks, self.blocks), self.rows, :]
        return w.reshape(self.half, self.half)

    def cols(self, j):
        return slice(j * self.half, (j + 1) * self.half)

    def vec(self, ref, j):
        return ref[:, pl.ds(pl.multiple_of(self.index[j] * self.half, self.half), self.half)]

    def apply(self, xs, j):
        return mm(xs[0], self.block(0, j)) + mm(xs[1], self.block(1, j))


def own_columns_kernel(t_own, t_oth, v_own, v_oth, l_own, l_oth, w_own, b1,
                       t2_own, aux):
    walkers = v_own.shape[0]
    mine, per, half = t2_own.shape
    c = lax.axis_index("feat")
    base = c * mine
    one = Halves(c, half, w_own, None, 0)
    vl = [jnp.concatenate([v[...], l[pl.ds(base, mine), :]], axis=0)
          for v, l in ((v_own, l_own), (v_oth, l_oth))]
    pre = one.apply(vl, 0)
    aux[:walkers, :] = jnp.tanh(pre[:walkers] + one.vec(b1, 0))
    aux[walkers:walkers + mine, :] = pre[walkers:]
    h1 = aux[pl.ds(base, mine), :]
    slope = 1.0 - h1 * h1
    for g in range(mine // GROUP):
        lo, hi = g * GROUP, (g + 1) * GROUP
        ts = [t[pl.ds(base + lo, GROUP)].reshape(GROUP * per, half) for t in (t_own, t_oth)]
        g1 = one.apply(ts, 0).reshape(GROUP, per, half)
        aux[walkers + mine + lo:walkers + mine + hi, :] = jnp.sum(g1 * g1, axis=1)
        t2_own[lo:hi] = (g1 * slope[lo:hi, None, :]).astype(BF16)


def rest_kernel(t_own, t_oth, t2_own, aux, v_own, v_oth, l_own, l_oth, w_own, w_oth, b1, b2, rd,
                amp_out, grad_out, s_out, h_sc, c1_sc, c2_sc):
    walkers = v_own.shape[0]
    mine, per, half = t2_own.shape
    c = lax.axis_index("feat")
    first_z = lax.axis_index("tangent") == 0
    base = c * mine
    one = Halves(c, half, w_own, w_oth, 0)
    two = Halves(c, half, w_own, w_oth, 1)
    vl = [jnp.concatenate([v[...], l[pl.ds(base, mine), :]], axis=0)
          for v, l in ((v_own, l_own), (v_oth, l_oth))]
    pre = one.apply(vl, 1)
    hid = jnp.tanh(pre[:walkers] + one.vec(b1, 1))
    h_sc[:walkers, one.cols(0)] = aux[:walkers, :]
    h_sc[:walkers, one.cols(1)] = hid
    lapin = [aux[walkers:walkers + mine, :], pre[walkers:]]
    value = [aux[:walkers, :].astype(BF16), hid.astype(BF16)]
    amp = None
    for j in (0, 1):
        hid = jnp.tanh(two.apply(value, j) + two.vec(b2, j))
        h_sc[walkers:, two.cols(j)] = hid
        term = two.vec(rd, j) * hid
        amp = term if amp is None else amp + term
    amp_out[...] = jnp.sum(amp[None], axis=-1)
    h1 = h_sc[pl.ds(base, mine), :]
    h2 = h_sc[pl.ds(walkers + base, mine), :]
    slope1 = 1.0 - h1 * h1
    slope2 = 1.0 - h2 * h2
    rs = [two.vec(rd, j) * slope2[:, two.cols(j)] for j in (0, 1)]
    for g in range(mine // GROUP):
        lo, hi = g * GROUP, (g + 1) * GROUP
        ts = [t[pl.ds(base + lo, GROUP)].reshape(GROUP * per, half) for t in (t_own, t_oth)]
        g1 = one.apply(ts, 1).reshape(GROUP, per, half)
        c1_sc[lo:hi, :] = jnp.sum(g1 * g1, axis=1)
        t2 = [t2_own[lo:hi].reshape(GROUP * per, half),
              (g1 * slope1[lo:hi, None, one.cols(1)]).astype(BF16).reshape(GROUP * per, half)]
        prod = None
        for j in (0, 1):
            g2 = two.apply(t2, j).reshape(GROUP, per, half)
            c2_sc[lo:hi, two.cols(j)] = jnp.sum(g2 * g2, axis=1)
            term = g2 * rs[j][lo:hi, None, :]
            prod = term if prod is None else prod + term
        grad_out[lo:hi, :] = jnp.sum(prod, axis=-1)
    curv = [aux[walkers + mine:, :], c1_sc[...]]
    laps = []
    for j in (0, 1):
        s1, h = slope1[:, one.cols(j)], h1[:, one.cols(j)]
        lap = jnp.where(first_z, s1 * lapin[j], 0.0) + (-2.0 * h * s1) * curv[j]
        high = lap.astype(BF16)
        laps.append(jnp.concatenate([high, (lap - high.astype(F32)).astype(BF16)], axis=0))
    total = None
    for j in (0, 1):
        both = two.apply(laps, j)
        h = h2[:, two.cols(j)]
        term = rs[j] * (both[:mine] + both[mine:] + (-2.0 * h) * c2_sc[:, two.cols(j)])
        total = term if total is None else total + term
    gr = grad_out[...]
    row = jnp.sum(total[None], axis=-1) + jnp.sum((gr * gr)[None], axis=-1)
    pair = jnp.concatenate([row, row], axis=1)
    lane = lax.broadcasted_iota(jnp.int32, pair.shape, 1)
    pair = jnp.where((lane >= base) & (lane < base + mine), pair, 0.0)
    s_out[...] = jnp.zeros_like(s_out)
    s_out[:, :walkers] = jnp.broadcast_to(pair, (s_out.shape[0], walkers))


def join_kernel(sums, grad, g_oth, amp, amp_out, grad_out, kin_out):
    mine = grad.shape[0]
    walkers = amp.shape[1]
    c = lax.axis_index("feat")
    amp_out[...] = amp[...]
    grad_out[pl.ds(c * mine, mine), :] = grad[...]
    grad_out[pl.ds((1 - c) * mine, mine), :] = g_oth[...]
    kin_out[...] = -0.5 * sums[:, :walkers]


def per_device(value_in, tang_in, lap_in, w_first, b_first, w_second, b_second, readout):
    walkers, half = value_in.shape
    per = tang_in.shape[1]
    n_z, n_c, n_w = lax.axis_size("tangent"), lax.axis_size("feat"), lax.axis_size("walker")
    mine = walkers // n_c
    peers = n_z * n_c
    rows = w_first.shape[0]
    swap = [(0, 1), (1, 0)]

    v_oth = lax.ppermute(value_in, "feat", swap)
    l_oth = lax.ppermute(lap_in, "feat", swap)
    t_oth = lax.ppermute(tang_in, "feat", swap)
    pair = jnp.concatenate([w_first, w_second], axis=0).reshape(2 * rows, n_c, half)
    piece = jnp.transpose(pair, (1, 0, 2))
    sent = jnp.broadcast_to(piece[None], (n_z, n_c, 2 * rows, half)).reshape(peers, 2 * rows, half)
    got = lax.all_to_all(sent, ("tangent", "feat"), 0, 0, tiled=True)
    got = jnp.transpose(got.reshape(peers, 2, rows, half), (1, 0, 2, 3)).reshape(2 * peers * rows, half)
    w_own = lax.all_to_all(jnp.broadcast_to(got[None], (n_w,) + got.shape), "walker", 0, 0, tiled=True)
    w_oth = lax.ppermute(w_own, "feat", swap)

    vm = pl.BlockSpec(memory_space=pltpu.VMEM)
    width = 2 * half
    params = pltpu.CompilerParams(vmem_limit_bytes=24 * 1024 * 1024)
    b1, b2, rd = b_first[None], b_second[None], readout[None]
    t2_own, aux = pl.pallas_call(
        own_columns_kernel,
        out_shape=(
            jax.ShapeDtypeStruct((mine, per, half), BF16),
            jax.ShapeDtypeStruct((walkers + 2 * mine, half), F32),
        ),
        in_specs=[vm] * 8,
        out_specs=(vm, vm),
        compiler_params=params,
        cost_estimate=pl.CostEstimate(flops=mine * per * width * width, bytes_accessed=1 << 22, transcendentals=0),
        name="own_columns",
    )(tang_in, t_oth, value_in, v_oth, lap_in, l_oth, w_own, b1)
    amp, grad, part = pl.pallas_call(
        rest_kernel,
        out_shape=(
            jax.ShapeDtypeStruct((1, walkers), F32),
            jax.ShapeDtypeStruct((mine, per), F32),
            jax.ShapeDtypeStruct((peers, LANES), F32),
        ),
        in_specs=[vm] * 13,
        out_specs=(vm, vm, vm),
        scratch_shapes=[
            pltpu.VMEM((2 * walkers, width), F32),
            pltpu.VMEM((mine, half), F32),
            pltpu.VMEM((mine, width), F32),
        ],
        compiler_params=params,
        cost_estimate=pl.CostEstimate(flops=3 * mine * per * width * width, bytes_accessed=1 << 22, transcendentals=0),
        name="rest",
    )(tang_in, t_oth, t2_own, aux, value_in, v_oth, lap_in, l_oth, w_own, w_oth, b1, b2, rd)

    g_oth = lax.ppermute(grad, "feat", swap)
    sums = lax.all_to_all(part.reshape(peers, 1, LANES), ("tangent", "feat"), 0, 0, tiled=True)
    total = jnp.sum(sums, axis=0)
    amp, gradient, kinetic = pl.pallas_call(
        join_kernel,
        out_shape=(
            jax.ShapeDtypeStruct((1, walkers), F32),
            jax.ShapeDtypeStruct((walkers, per), F32),
            jax.ShapeDtypeStruct((1, walkers), F32),
        ),
        in_specs=[vm] * 4,
        out_specs=(vm, vm, vm),
        compiler_params=pltpu.CompilerParams(vmem_limit_bytes=2 * 1024 * 1024),
        name="join",
    )(total, grad, g_oth, amp)
    return amp.reshape(walkers), gradient, kinetic.reshape(walkers)


def solution(mesh):
    placed = (
        P("walker", "feat"),
        P("walker", "tangent", "feat"),
        P("walker", "feat"),
        P(("walker", "tangent", "feat"), None),
        P(),
        P(("walker", "tangent", "feat"), None),
        P(),
        P(),
    )

    return jax.shard_map(
        per_device,
        mesh=mesh,
        in_specs=placed,
        out_specs=(P("walker"), P("walker", "tangent"), P("walker")),
        check_vma=False,
    )
```

```python
import math

import jax
import jax.numpy as jnp
from jax import lax
from jax.experimental import pallas as pl
from jax.experimental.pallas import tpu as pltpu
from jax.sharding import PartitionSpec as P

BF16, F32 = jnp.bfloat16, jnp.float32
GROUP = 8
LANES = 128


def mm(a, b):
    return jnp.dot(a, b, preferred_element_type=F32)


class Halves:
    def __init__(self, c, half, w_own, w_oth, layer):
        self.index = (c, 1 - c)
        self.half = half
        self.weights = (w_own, w_oth)
        self.blocks = w_own.shape[0] // 2
        rows = w_own.shape[1] // 2
        self.rows = slice(layer * rows, (layer + 1) * rows)

    def block(self, k, j):
        w = self.weights[j][pl.ds(self.index[k] * self.blocks, self.blocks), self.rows, :]
        return w.reshape(self.half, self.half)

    def cols(self, j):
        return slice(j * self.half, (j + 1) * self.half)

    def vec(self, ref, j):
        return ref[:, pl.ds(pl.multiple_of(self.index[j] * self.half, self.half), self.half)]

    def apply(self, xs, j):
        return mm(xs[0], self.block(0, j)) + mm(xs[1], self.block(1, j))

    def apply_wide(self, xs, j):
        cut = xs[0].shape[0] // 2
        return jnp.concatenate([self.apply([x[:cut] for x in xs], j), self.apply([x[cut:] for x in xs], j)], axis=0)


def natural_order(blocks, out):
    x = lax.axis_index("wx") + len(blocks)
    for d, block in enumerate(blocks):
        out[lax.rem(x - d, len(blocks))] = block[...]


def fetch_kernel(t, v, l, b1, b2, rd, t_mine, vl_own, vecs, sems):
    walkers = v.shape[0]
    rows = t_mine.shape[0]
    mine = lax.axis_index("feat") * rows
    copies = [
        pltpu.make_async_copy(t.at[pl.ds(mine, rows)], t_mine, sems.at[0]),
        pltpu.make_async_copy(v, vl_own.at[pl.ds(0, walkers)], sems.at[1]),
        pltpu.make_async_copy(l, vl_own.at[pl.ds(walkers, walkers)], sems.at[2]),
    ]
    for n, b in enumerate((b1, b2, rd)):
        copies.append(pltpu.make_async_copy(b, vecs.at[n], sems.at[3 + n]))
    for copy in copies:
        copy.start()
    for copy in copies:
        copy.wait()


def block_kernel(got, out):
    peers, layers, rows, _ = got.shape
    for n in range(layers):
        for k in range(peers):
            at = (n * peers + k) * rows
            out[at:at + rows, :] = got[k, n]


def prep_kernel(w1, w2, v, l, sent, pack, w_buf, sems):
    walkers, half = v.shape
    copies = [
        pltpu.make_async_copy(w1, w_buf.at[0], sems.at[0]),
        pltpu.make_async_copy(w2, w_buf.at[1], sems.at[1]),
        pltpu.make_async_copy(v, pack.at[pl.ds(0, walkers)], sems.at[2]),
        pltpu.make_async_copy(l, pack.at[pl.ds(walkers, walkers)], sems.at[3]),
    ]
    for copy in copies:
        copy.start()
    copies[0].wait()
    copies[1].wait()
    for n in (0, 1):
        for k in range(sent.shape[0]):
            h = k % 2
            sent[k, n] = w_buf[n, :, h * half:(h + 1) * half]
    for copy in copies[2:]:
        copy.wait()


def own_columns_kernel(t_own, t_oth, vl_own, vl_oth, w_0, w_1, w_2, w_3, vecs, t2_own, g2_part, aux, w_own):
    walkers = vl_own.shape[0] // 2
    b1, _, _ = (vecs.at[n] for n in range(3))
    mine, per, half = t2_own.shape
    c = lax.axis_index("feat")
    base = c * mine
    natural_order((w_0, w_1, w_2, w_3), w_own)
    one = Halves(c, half, w_own, None, 0)
    two = Halves(c, half, w_own, None, 1)
    aux[:walkers, :] = jnp.tanh(one.apply((vl_own[:walkers, :], vl_oth[:walkers, :]), 0) + one.vec(b1, 0))
    h1 = aux[pl.ds(base, mine), :]
    slope = 1.0 - h1 * h1
    for g in range(mine // GROUP):
        lo, hi = g * GROUP, (g + 1) * GROUP
        ts = (t_own[lo * per:hi * per, :], t_oth[pl.ds((base + lo) * per, GROUP * per), :])
        g1 = one.apply_wide(ts, 0).reshape(GROUP, per, half)
        aux[walkers + lo:walkers + hi, :] = jnp.sum(g1 * g1, axis=1)
        t2 = (g1 * slope[lo:hi, None, :]).astype(BF16)
        t2_own[lo:hi] = t2
        g2_part[lo:hi] = mm(t2.reshape(GROUP * per, half), two.block(0, 0)).reshape(GROUP, per, half)


def rest_kernel(t_own, t_oth, t2_own, g2_part, aux, vl_own, vl_oth, w_own, w_0, w_1, w_2, w_3, vecs,
                amp_out, grad_out, s_out, h_sc, c1_sc, c2_sc, w_oth):
    walkers = vl_own.shape[0] // 2
    b1, b2, rd = (vecs.at[n] for n in range(3))
    mine, per, half = t2_own.shape
    c = lax.axis_index("feat")
    first_z = lax.axis_index("tangent") == 0
    base = c * mine
    natural_order((w_0, w_1, w_2, w_3), w_oth)
    one = Halves(c, half, w_own, w_oth, 0)
    two = Halves(c, half, w_own, w_oth, 1)
    vs = (vl_own[:walkers, :], vl_oth[:walkers, :])
    ls = [vl[pl.ds(walkers + base, mine), :] for vl in (vl_own, vl_oth)]
    vl = [jnp.concatenate([v, l], axis=0) for v, l in zip(vs, ls)]
    pre = one.apply(vl, 1)
    hid = jnp.tanh(pre[:walkers] + one.vec(b1, 1))
    h_sc[:walkers, one.cols(0)] = aux[:walkers, :]
    h_sc[:walkers, one.cols(1)] = hid
    lapin = [one.apply(ls, 0), pre[walkers:]]
    value = [aux[:walkers, :].astype(BF16), hid.astype(BF16)]
    amp = None
    for j in (0, 1):
        hid = jnp.tanh(two.apply(value, j) + two.vec(b2, j))
        h_sc[walkers:, two.cols(j)] = hid
        term = two.vec(rd, j) * hid
        amp = term if amp is None else amp + term
    amp_out[...] = jnp.sum(amp[None], axis=-1)
    h1 = h_sc[pl.ds(base, mine), :]
    h2 = h_sc[pl.ds(walkers + base, mine), :]
    slope1 = 1.0 - h1 * h1
    slope2 = 1.0 - h2 * h2
    rs = [two.vec(rd, j) * slope2[:, two.cols(j)] for j in (0, 1)]
    for g in range(mine // GROUP):
        lo, hi = g * GROUP, (g + 1) * GROUP
        ts = (t_own[lo * per:hi * per, :], t_oth[pl.ds((base + lo) * per, GROUP * per), :])
        g1 = one.apply_wide(ts, 1).reshape(GROUP, per, half)
        c1_sc[lo:hi, :] = jnp.sum(g1 * g1, axis=1)
        t2 = [t2_own[lo:hi].reshape(GROUP * per, half),
              (g1 * slope1[lo:hi, None, one.cols(1)]).astype(BF16).reshape(GROUP * per, half)]
        prod = None
        for j in (0, 1):
            if j == 0:
                g2 = g2_part[lo:hi] + mm(t2[1], two.block(1, 0)).reshape(GROUP, per, half)
            else:
                g2 = two.apply(t2, j).reshape(GROUP, per, half)
            c2_sc[lo:hi, two.cols(j)] = jnp.sum(g2 * g2, axis=1)
            term = g2 * rs[j][lo:hi, None, :]
            prod = term if prod is None else prod + term
        grad_out[lo:hi, :] = jnp.sum(prod, axis=-1)
    curv = [aux[walkers:, :], c1_sc[...]]
    laps = []
    for j in (0, 1):
        s1, h = slope1[:, one.cols(j)], h1[:, one.cols(j)]
        lap = jnp.where(first_z, s1 * lapin[j], 0.0) + (-2.0 * h * s1) * curv[j]
        high = lap.astype(BF16)
        laps.append(jnp.concatenate([high, (lap - high.astype(F32)).astype(BF16)], axis=0))
    total = None
    for j in (0, 1):
        both = two.apply(laps, j)
        h = h2[:, two.cols(j)]
        term = rs[j] * (both[:mine] + both[mine:] + (-2.0 * h) * c2_sc[:, two.cols(j)])
        total = term if total is None else total + term
    gr = grad_out[...]
    row = jnp.sum(total[None], axis=-1) + jnp.sum((gr * gr)[None], axis=-1)
    pair = jnp.concatenate([row, row], axis=1)
    lane = lax.broadcasted_iota(jnp.int32, pair.shape, 1)
    pair = jnp.where((lane >= base) & (lane < base + mine), pair, 0.0)
    s_out[...] = jnp.zeros_like(s_out)
    s_out[:, :walkers] = jnp.broadcast_to(pair, (s_out.shape[0], walkers))


def join_kernel(sums, grad, g_oth, amp, amp_out, grad_out, kin_out):
    mine = grad.shape[0]
    walkers = amp.shape[1]
    c = lax.axis_index("feat")
    amp_out[...] = amp[...]
    grad_out[pl.ds(c * mine, mine), :] = grad[...]
    grad_out[pl.ds((1 - c) * mine, mine), :] = g_oth[...]
    kin_out[...] = -0.5 * sums[:, :walkers]


def in_hbm(x):
    return pltpu.with_memory_space_constraint(x, pltpu.HBM)


def per_device(value_in, tang_in, lap_in, w_first, b_first, w_second, b_second, readout):
    walkers, half = value_in.shape
    per = tang_in.shape[1]
    n_z, n_c = lax.axis_size("tangent"), lax.axis_size("feat")
    n_x, n_y = lax.axis_size("wx"), lax.axis_size("wy")
    mine = walkers // n_c
    peers = n_z * n_c
    rows = w_first.shape[0]
    swap = [(0, 1), (1, 0)]

    flat = tang_in.reshape(walkers * per, half)
    vm = pl.BlockSpec(memory_space=pltpu.VMEM)
    hbm = pl.BlockSpec(memory_space=pltpu.HBM)
    params = pltpu.CompilerParams(vmem_limit_bytes=24 * 1024 * 1024)
    sent, pack = pl.pallas_call(
        prep_kernel,
        out_shape=(
            jax.ShapeDtypeStruct((n_y * peers, 2, rows, half), BF16),
            jax.ShapeDtypeStruct((2 * walkers, half), BF16),
        ),
        in_specs=[hbm] * 4,
        out_specs=(vm, vm),
        scratch_shapes=[pltpu.VMEM((2, rows, n_c * half), BF16), pltpu.SemaphoreType.DMA((4,))],
        compiler_params=params,
        name="prep",
    )(*(in_hbm(x) for x in (w_first, w_second, value_in, lap_in)))
    vl_oth = lax.ppermute(pack, "feat", swap)
    t_oth = lax.ppermute(flat, "feat", swap)
    got = lax.all_to_all(sent, ("wy", "tangent", "feat"), 0, 0, tiled=True)
    block = pl.pallas_call(
        block_kernel,
        out_shape=jax.ShapeDtypeStruct((2 * n_y * peers * rows, half), BF16),
        in_specs=[vm],
        out_specs=vm,
        compiler_params=params,
        name="block",
    )(got)
    near, far = [block] * n_x, [None] * n_x
    for d in (2, 1, 3):
        near[d] = lax.ppermute(block, "wx", [(i, (i + d) % n_x) for i in range(n_x)])
    for d in (0, 2, 1, 3):
        far[d] = lax.ppermute(near[d], "feat", swap)

    width = 2 * half
    t_own, vl_own, vecs = pl.pallas_call(
        fetch_kernel,
        out_shape=(
            jax.ShapeDtypeStruct((mine * per, half), BF16),
            jax.ShapeDtypeStruct((2 * walkers, half), BF16),
            jax.ShapeDtypeStruct((3, 1, width), F32),
        ),
        in_specs=[hbm] * 6,
        out_specs=(vm, vm, vm),
        scratch_shapes=[pltpu.SemaphoreType.DMA((6,))],
        compiler_params=params,
        name="fetch",
    )(*(in_hbm(x) for x in (flat, value_in, lap_in, b_first[None], b_second[None], readout[None])))
    t2_own, g2_part, aux, w_own = pl.pallas_call(
        own_columns_kernel,
        out_shape=(
            jax.ShapeDtypeStruct((mine, per, half), BF16),
            jax.ShapeDtypeStruct((mine, per, half), F32),
            jax.ShapeDtypeStruct((walkers + mine, half), F32),
            jax.ShapeDtypeStruct((n_x,) + block.shape, BF16),
        ),
        in_specs=[vm] * 9,
        out_specs=(vm, vm, vm, vm),
        compiler_params=params,
        cost_estimate=pl.CostEstimate(flops=mine * per * width * width, bytes_accessed=1 << 22, transcendentals=0),
        name="own_columns",
    )(t_own, t_oth, vl_own, vl_oth, *near, vecs)
    amp, grad, part = pl.pallas_call(
        rest_kernel,
        out_shape=(
            jax.ShapeDtypeStruct((1, walkers), F32),
            jax.ShapeDtypeStruct((mine, per), F32),
            jax.ShapeDtypeStruct((peers, LANES), F32),
        ),
        in_specs=[vm] * 13,
        out_specs=(vm, vm, vm),
        scratch_shapes=[
            pltpu.VMEM((2 * walkers, width), F32),
            pltpu.VMEM((mine, half), F32),
            pltpu.VMEM((mine, width), F32),
            pltpu.VMEM((n_x,) + block.shape, BF16),
        ],
        compiler_params=params,
        cost_estimate=pl.CostEstimate(flops=3 * mine * per * width * width, bytes_accessed=1 << 22, transcendentals=0),
        name="rest",
    )(t_own, t_oth, t2_own, g2_part, aux, vl_own, vl_oth, w_own, *far, vecs)

    g_oth = lax.ppermute(grad, "feat", swap)
    sums = lax.all_to_all(part.reshape(peers, 1, LANES), ("tangent", "feat"), 0, 0, tiled=True)
    total = jnp.sum(sums, axis=0)
    amp, gradient, kinetic = pl.pallas_call(
        join_kernel,
        out_shape=(
            jax.ShapeDtypeStruct((1, walkers), F32),
            jax.ShapeDtypeStruct((walkers, per), F32),
            jax.ShapeDtypeStruct((1, walkers), F32),
        ),
        in_specs=[vm] * 4,
        out_specs=(vm, vm, vm),
        compiler_params=pltpu.CompilerParams(vmem_limit_bytes=2 * 1024 * 1024),
        name="join",
    )(total, grad, g_oth, amp)
    return amp.reshape(walkers), gradient, kinetic.reshape(walkers)


def solution(mesh):
    walker, tangent, feat = mesh.devices.shape
    side = math.isqrt(walker)
    mesh = jax.sharding.Mesh(mesh.devices.reshape(side, side, tangent, feat), ("wx", "wy", "tangent", "feat"))
    placed = (
        P(("wx", "wy"), "feat"),
        P(("wx", "wy"), "tangent", "feat"),
        P(("wx", "wy"), "feat"),
        P(("wx", "wy", "tangent", "feat"), None),
        P(),
        P(("wx", "wy", "tangent", "feat"), None),
        P(),
        P(),
    )

    return jax.shard_map(
        per_device,
        mesh=mesh,
        in_specs=placed,
        out_specs=(P(("wx", "wy")), P(("wx", "wy"), "tangent"), P(("wx", "wy"))),
        check_vma=False,
    )
```

```python
import math

import jax
import jax.numpy as jnp
from jax import lax
from jax.experimental import pallas as pl
from jax.experimental.pallas import tpu as pltpu
from jax.sharding import PartitionSpec as P

BF16, F32 = jnp.bfloat16, jnp.float32
GROUP = 8
LANES = 128


def mm(a, b):
    return jnp.dot(a, b, preferred_element_type=F32)


class Halves:
    def __init__(self, c, half, w_own, w_oth, layer):
        self.index = (c, 1 - c)
        self.half = half
        self.weights = (w_own, w_oth)
        self.blocks = w_own.shape[0] // 2
        rows = w_own.shape[1] // 2
        self.rows = slice(layer * rows, (layer + 1) * rows)

    def block(self, k, j):
        w = self.weights[j][pl.ds(self.index[k] * self.blocks, self.blocks), self.rows, :]
        return w.reshape(self.half, self.half)

    def cols(self, j):
        return slice(j * self.half, (j + 1) * self.half)

    def vec(self, ref, j):
        return ref[:, pl.ds(pl.multiple_of(self.index[j] * self.half, self.half), self.half)]

    def apply(self, xs, j):
        return mm(xs[0], self.block(0, j)) + mm(xs[1], self.block(1, j))

    def apply_wide(self, xs, j):
        cut = xs[0].shape[0] // 2
        return jnp.concatenate([self.apply([x[:cut] for x in xs], j), self.apply([x[cut:] for x in xs], j)], axis=0)


def natural_order(blocks, out):
    x = lax.axis_index("wx") + len(blocks)
    for d, block in enumerate(blocks):
        out[lax.rem(x - d, len(blocks))] = block[...]


def fetch_kernel(t, v, l, b1, b2, rd, t_mine, vl_own, vecs, sems):
    walkers = v.shape[0]
    rows = t_mine.shape[0]
    mine = lax.axis_index("feat") * rows
    copies = [
        pltpu.make_async_copy(t.at[pl.ds(mine, rows)], t_mine, sems.at[0]),
        pltpu.make_async_copy(v, vl_own.at[pl.ds(0, walkers)], sems.at[1]),
        pltpu.make_async_copy(l, vl_own.at[pl.ds(walkers, walkers)], sems.at[2]),
    ]
    for n, b in enumerate((b1, b2, rd)):
        copies.append(pltpu.make_async_copy(b, vecs.at[n], sems.at[3 + n]))
    for copy in copies:
        copy.start()
    for copy in copies:
        copy.wait()


def block_kernel(got, out):
    peers, layers, rows, _ = got.shape
    for n in range(layers):
        for k in range(peers):
            at = (n * peers + k) * rows
            out[at:at + rows, :] = got[k, n]


def prep_kernel(w1, w2, sent, w_buf, sems):
    half = sent.shape[3]
    copies = [pltpu.make_async_copy(w, w_buf.at[n], sems.at[n]) for n, w in enumerate((w1, w2))]
    for copy in copies:
        copy.start()
    for n, copy in enumerate(copies):
        copy.wait()
        for k in range(sent.shape[0]):
            h = k % 2
            sent[k, n] = w_buf[n, :, h * half:(h + 1) * half]


def own_columns_kernel(t_own, t_oth, vl_own, vl_oth, w_0, w_1, w_2, w_3, vecs, t2_own, g2_part, aux, w_own):
    walkers = vl_own.shape[0] // 2
    b1, _, _ = (vecs.at[n] for n in range(3))
    mine, per, half = t2_own.shape
    c = lax.axis_index("feat")
    base = c * mine
    natural_order((w_0, w_1, w_2, w_3), w_own)
    one = Halves(c, half, w_own, None, 0)
    two = Halves(c, half, w_own, None, 1)
    aux[:walkers, :] = jnp.tanh(one.apply((vl_own[:walkers, :], vl_oth[:walkers, :]), 0) + one.vec(b1, 0))
    h1 = aux[pl.ds(base, mine), :]
    slope = 1.0 - h1 * h1
    for g in range(mine // GROUP):
        lo, hi = g * GROUP, (g + 1) * GROUP
        ts = (t_own[lo * per:hi * per, :], t_oth[pl.ds((base + lo) * per, GROUP * per), :])
        g1 = one.apply_wide(ts, 0).reshape(GROUP, per, half)
        aux[walkers + lo:walkers + hi, :] = jnp.sum(g1 * g1, axis=1)
        t2 = (g1 * slope[lo:hi, None, :]).astype(BF16)
        t2_own[lo:hi] = t2
        g2_part[lo:hi] = mm(t2.reshape(GROUP * per, half), two.block(0, 0)).reshape(GROUP, per, half)


def rest_kernel(t_own, t_oth, t2_own, g2_part, aux, vl_own, vl_oth, w_own, w_0, w_1, w_2, w_3, vecs,
                amp_out, grad_out, s_out, h_sc, c1_sc, c2_sc, w_oth):
    walkers = vl_own.shape[0] // 2
    b1, b2, rd = (vecs.at[n] for n in range(3))
    mine, per, half = t2_own.shape
    c = lax.axis_index("feat")
    first_z = lax.axis_index("tangent") == 0
    base = c * mine
    natural_order((w_0, w_1, w_2, w_3), w_oth)
    one = Halves(c, half, w_own, w_oth, 0)
    two = Halves(c, half, w_own, w_oth, 1)
    vs = (vl_own[:walkers, :], vl_oth[:walkers, :])
    ls = [vl[pl.ds(walkers + base, mine), :] for vl in (vl_own, vl_oth)]
    vl = [jnp.concatenate([v, l], axis=0) for v, l in zip(vs, ls)]
    pre = one.apply(vl, 1)
    hid = jnp.tanh(pre[:walkers] + one.vec(b1, 1))
    h_sc[:walkers, one.cols(0)] = aux[:walkers, :]
    h_sc[:walkers, one.cols(1)] = hid
    lapin = [one.apply(ls, 0), pre[walkers:]]
    value = [aux[:walkers, :].astype(BF16), hid.astype(BF16)]
    amp = None
    for j in (0, 1):
        hid = jnp.tanh(two.apply(value, j) + two.vec(b2, j))
        h_sc[walkers:, two.cols(j)] = hid
        term = two.vec(rd, j) * hid
        amp = term if amp is None else amp + term
    amp_out[...] = jnp.sum(amp[None], axis=-1)
    h1 = h_sc[pl.ds(base, mine), :]
    h2 = h_sc[pl.ds(walkers + base, mine), :]
    slope1 = 1.0 - h1 * h1
    slope2 = 1.0 - h2 * h2
    rs = [two.vec(rd, j) * slope2[:, two.cols(j)] for j in (0, 1)]
    for g in range(mine // GROUP):
        lo, hi = g * GROUP, (g + 1) * GROUP
        ts = (t_own[lo * per:hi * per, :], t_oth[pl.ds((base + lo) * per, GROUP * per), :])
        g1 = one.apply_wide(ts, 1).reshape(GROUP, per, half)
        c1_sc[lo:hi, :] = jnp.sum(g1 * g1, axis=1)
        t2 = [t2_own[lo:hi].reshape(GROUP * per, half),
              (g1 * slope1[lo:hi, None, one.cols(1)]).astype(BF16).reshape(GROUP * per, half)]
        prod = None
        for j in (0, 1):
            if j == 0:
                g2 = g2_part[lo:hi] + mm(t2[1], two.block(1, 0)).reshape(GROUP, per, half)
            else:
                g2 = two.apply(t2, j).reshape(GROUP, per, half)
            c2_sc[lo:hi, two.cols(j)] = jnp.sum(g2 * g2, axis=1)
            term = g2 * rs[j][lo:hi, None, :]
            prod = term if prod is None else prod + term
        grad_out[lo:hi, :] = jnp.sum(prod, axis=-1)
    curv = [aux[walkers:, :], c1_sc[...]]
    laps = []
    for j in (0, 1):
        s1, h = slope1[:, one.cols(j)], h1[:, one.cols(j)]
        lap = jnp.where(first_z, s1 * lapin[j], 0.0) + (-2.0 * h * s1) * curv[j]
        high = lap.astype(BF16)
        laps.append(jnp.concatenate([high, (lap - high.astype(F32)).astype(BF16)], axis=0))
    total = None
    for j in (0, 1):
        both = two.apply(laps, j)
        h = h2[:, two.cols(j)]
        term = rs[j] * (both[:mine] + both[mine:] + (-2.0 * h) * c2_sc[:, two.cols(j)])
        total = term if total is None else total + term
    gr = grad_out[...]
    row = jnp.sum(total[None], axis=-1) + jnp.sum((gr * gr)[None], axis=-1)
    pair = jnp.concatenate([row, row], axis=1)
    lane = lax.broadcasted_iota(jnp.int32, pair.shape, 1)
    pair = jnp.where((lane >= base) & (lane < base + mine), pair, 0.0)
    s_out[...] = jnp.zeros_like(s_out)
    s_out[:, :walkers] = jnp.broadcast_to(pair, (s_out.shape[0], walkers))


def join_kernel(sums, grad, g_oth, amp, amp_out, grad_out, kin_out):
    mine = grad.shape[0]
    walkers = amp.shape[1]
    c = lax.axis_index("feat")
    amp_out[...] = amp[...]
    grad_out[pl.ds(c * mine, mine), :] = grad[...]
    grad_out[pl.ds((1 - c) * mine, mine), :] = g_oth[...]
    kin_out[...] = -0.5 * sums[:, :walkers]


def in_hbm(x):
    return pltpu.with_memory_space_constraint(x, pltpu.HBM)


def per_device(value_in, tang_in, lap_in, w_first, b_first, w_second, b_second, readout):
    walkers, half = value_in.shape
    per = tang_in.shape[1]
    n_z, n_c = lax.axis_size("tangent"), lax.axis_size("feat")
    n_x, n_y = lax.axis_size("wx"), lax.axis_size("wy")
    mine = walkers // n_c
    peers = n_z * n_c
    rows = w_first.shape[0]
    swap = [(0, 1), (1, 0)]

    flat = tang_in.reshape(walkers * per, half)
    vm = pl.BlockSpec(memory_space=pltpu.VMEM)
    hbm = pl.BlockSpec(memory_space=pltpu.HBM)
    params = pltpu.CompilerParams(vmem_limit_bytes=24 * 1024 * 1024)
    sent = pl.pallas_call(
        prep_kernel,
        out_shape=jax.ShapeDtypeStruct((n_y * peers, 2, rows, half), BF16),
        in_specs=[hbm] * 2,
        out_specs=vm,
        scratch_shapes=[pltpu.VMEM((2, rows, n_c * half), BF16), pltpu.SemaphoreType.DMA((2,))],
        compiler_params=params,
        name="prep",
    )(in_hbm(w_first), in_hbm(w_second))
    t_oth = lax.ppermute(flat, "feat", swap)
    got = lax.all_to_all(sent, ("wy", "tangent", "feat"), 0, 0, tiled=True)
    block = pl.pallas_call(
        block_kernel,
        out_shape=jax.ShapeDtypeStruct((2 * n_y * peers * rows, half), BF16),
        in_specs=[vm],
        out_specs=vm,
        compiler_params=params,
        name="block",
    )(got)
    near, far = [block] * n_x, [None] * n_x
    for d in (2, 1, 3):
        near[d] = lax.ppermute(block, "wx", [(i, (i + d) % n_x) for i in range(n_x)])
    for d in (0, 2, 1, 3):
        far[d] = lax.ppermute(near[d], "feat", swap)

    width = 2 * half
    t_own, vl_own, vecs = pl.pallas_call(
        fetch_kernel,
        out_shape=(
            jax.ShapeDtypeStruct((mine * per, half), BF16),
            jax.ShapeDtypeStruct((2 * walkers, half), BF16),
            jax.ShapeDtypeStruct((3, 1, width), F32),
        ),
        in_specs=[hbm] * 6,
        out_specs=(vm, vm, vm),
        scratch_shapes=[pltpu.SemaphoreType.DMA((6,))],
        compiler_params=params,
        name="fetch",
    )(*(in_hbm(x) for x in (flat, value_in, lap_in, b_first[None], b_second[None], readout[None])))
    vl_oth = lax.ppermute(vl_own, "feat", swap)
    t2_own, g2_part, aux, w_own = pl.pallas_call(
        own_columns_kernel,
        out_shape=(
            jax.ShapeDtypeStruct((mine, per, half), BF16),
            jax.ShapeDtypeStruct((mine, per, half), F32),
            jax.ShapeDtypeStruct((walkers + mine, half), F32),
            jax.ShapeDtypeStruct((n_x,) + block.shape, BF16),
        ),
        in_specs=[vm] * 9,
        out_specs=(vm, vm, vm, vm),
        compiler_params=params,
        cost_estimate=pl.CostEstimate(flops=mine * per * width * width, bytes_accessed=1 << 22, transcendentals=0),
        name="own_columns",
    )(t_own, t_oth, vl_own, vl_oth, *near, vecs)
    amp, grad, part = pl.pallas_call(
        rest_kernel,
        out_shape=(
            jax.ShapeDtypeStruct((1, walkers), F32),
            jax.ShapeDtypeStruct((mine, per), F32),
            jax.ShapeDtypeStruct((peers, LANES), F32),
        ),
        in_specs=[vm] * 13,
        out_specs=(vm, vm, vm),
        scratch_shapes=[
            pltpu.VMEM((2 * walkers, width), F32),
            pltpu.VMEM((mine, half), F32),
            pltpu.VMEM((mine, width), F32),
            pltpu.VMEM((n_x,) + block.shape, BF16),
        ],
        compiler_params=params,
        cost_estimate=pl.CostEstimate(flops=3 * mine * per * width * width, bytes_accessed=1 << 22, transcendentals=0),
        name="rest",
    )(t_own, t_oth, t2_own, g2_part, aux, vl_own, vl_oth, w_own, *far, vecs)

    g_oth = lax.ppermute(grad, "feat", swap)
    sums = lax.all_to_all(part.reshape(peers, 1, LANES), ("tangent", "feat"), 0, 0, tiled=True)
    total = jnp.sum(sums, axis=0)
    amp, gradient, kinetic = pl.pallas_call(
        join_kernel,
        out_shape=(
            jax.ShapeDtypeStruct((1, walkers), F32),
            jax.ShapeDtypeStruct((walkers, per), F32),
            jax.ShapeDtypeStruct((1, walkers), F32),
        ),
        in_specs=[vm] * 4,
        out_specs=(vm, vm, vm),
        compiler_params=pltpu.CompilerParams(vmem_limit_bytes=2 * 1024 * 1024),
        name="join",
    )(total, grad, g_oth, amp)
    return amp.reshape(walkers), gradient, kinetic.reshape(walkers)


def solution(mesh):
    walker, tangent, feat = mesh.devices.shape
    side = math.isqrt(walker)
    mesh = jax.sharding.Mesh(mesh.devices.reshape(side, side, tangent, feat), ("wx", "wy", "tangent", "feat"))
    placed = (
        P(("wx", "wy"), "feat"),
        P(("wx", "wy"), "tangent", "feat"),
        P(("wx", "wy"), "feat"),
        P(("wx", "wy", "tangent", "feat"), None),
        P(),
        P(("wx", "wy", "tangent", "feat"), None),
        P(),
        P(),
    )

    return jax.shard_map(
        per_device,
        mesh=mesh,
        in_specs=placed,
        out_specs=(P(("wx", "wy")), P(("wx", "wy"), "tangent"), P(("wx", "wy"))),
        check_vma=False,
    )
```

```python
import math

import jax
import jax.numpy as jnp
from jax import lax
from jax.experimental import pallas as pl
from jax.experimental.pallas import tpu as pltpu
from jax.sharding import PartitionSpec as P

BF16, F32 = jnp.bfloat16, jnp.float32
GROUP = 8
LANES = 128


def mm(a, b):
    return jnp.dot(a, b, preferred_element_type=F32)


def mm_wide(a, b):
    cut = a.shape[0] // 2
    return jnp.concatenate([mm(a[:cut], b), mm(a[cut:], b)], axis=0)


class Halves:
    def __init__(self, c, half, w_own, w_oth, layer):
        self.index = (c, 1 - c)
        self.half = half
        self.weights = (w_own, w_oth)
        self.blocks = w_own.shape[0] // 2
        self.layer = layer

    def block(self, k, j):
        w = self.weights[j][pl.ds(self.index[k] * self.blocks, self.blocks), self.layer]
        return w.reshape(self.half, self.half)

    def cols(self, j):
        return slice(j * self.half, (j + 1) * self.half)

    def vec(self, ref, j):
        return ref[:, pl.ds(pl.multiple_of(self.index[j] * self.half, self.half), self.half)]

    def apply(self, xs, j):
        return mm(xs[0], self.block(0, j)) + mm(xs[1], self.block(1, j))

    def apply_wide(self, xs, j):
        cut = xs[0].shape[0] // 2
        return jnp.concatenate([self.apply([x[:cut] for x in xs], j), self.apply([x[cut:] for x in xs], j)], axis=0)


def natural_order(blocks, out):
    y = lax.axis_index("wy") + len(blocks)
    n_x, layers, _, rows, _ = out.shape
    for d, block in enumerate(blocks):
        for n in range(layers):
            for k in range(n_x):
                at = (n * n_x + k) * rows
                out[k, n, lax.rem(y - d, len(blocks))] = block[at:at + rows, :]


def fetch_kernel(t, v, l, b1, b2, rd, t_mine, vl_own, vecs, sems):
    walkers = v.shape[0]
    rows = t_mine.shape[0]
    mine = lax.axis_index("feat") * rows
    copies = [
        pltpu.make_async_copy(t.at[pl.ds(mine, rows)], t_mine, sems.at[0]),
        pltpu.make_async_copy(v, vl_own.at[pl.ds(0, walkers)], sems.at[1]),
        pltpu.make_async_copy(l, vl_own.at[pl.ds(walkers, walkers)], sems.at[2]),
    ]
    for n, b in enumerate((b1, b2, rd)):
        copies.append(pltpu.make_async_copy(b, vecs.at[n], sems.at[3 + n]))
    for copy in copies:
        copy.start()
    for copy in copies:
        copy.wait()


def block_kernel(got, out):
    peers, layers, rows, _ = got.shape
    for n in range(layers):
        for k in range(peers):
            at = (n * peers + k) * rows
            out[at:at + rows, :] = got[k, n]


def prep_kernel(w1, w2, sent, w_buf, sems):
    half = sent.shape[3]
    copies = [pltpu.make_async_copy(w, w_buf.at[n], sems.at[n]) for n, w in enumerate((w1, w2))]
    for copy in copies:
        copy.start()
    for n, copy in enumerate(copies):
        copy.wait()
        for k in range(sent.shape[0]):
            h = k % 2
            sent[k, n] = w_buf[n, :, h * half:(h + 1) * half]


def own_columns_kernel(t_own, t_oth, vl_own, vl_oth, w_0, w_1, w_2, w_3, vecs, t2_own, g2_part, aux, w_own):
    walkers = vl_own.shape[0] // 2
    b1, _, _ = (vecs.at[n] for n in range(3))
    mine, per, half = t2_own.shape
    c = lax.axis_index("feat")
    base = c * mine
    natural_order((w_0, w_1, w_2, w_3), w_own)
    one = Halves(c, half, w_own, None, 0)
    two = Halves(c, half, w_own, None, 1)
    aux[:walkers, :] = jnp.tanh(one.apply((vl_own[:walkers, :], vl_oth[:walkers, :]), 0) + one.vec(b1, 0))
    h1 = aux[pl.ds(base, mine), :]
    slope = 1.0 - h1 * h1
    for g in range(mine // GROUP):
        lo, hi = g * GROUP, (g + 1) * GROUP
        ts = (t_own[lo * per:hi * per, :], t_oth[pl.ds((base + lo) * per, GROUP * per), :])
        g1 = one.apply_wide(ts, 0).reshape(GROUP, per, half)
        aux[walkers + lo:walkers + hi, :] = jnp.sum(g1 * g1, axis=1)
        t2 = (g1 * slope[lo:hi, None, :]).astype(BF16)
        t2_own[lo:hi] = t2
        g2_part[lo:hi] = mm_wide(t2.reshape(GROUP * per, half), two.block(0, 0)).reshape(GROUP, per, half)


def rest_kernel(t_own, t_oth, t2_own, g2_part, aux, vl_own, vl_oth, w_own, w_0, w_1, w_2, w_3, vecs,
                amp_out, grad_out, s_out, h_sc, c1_sc, c2_sc, w_oth):
    walkers = vl_own.shape[0] // 2
    b1, b2, rd = (vecs.at[n] for n in range(3))
    mine, per, half = t2_own.shape
    c = lax.axis_index("feat")
    first_z = lax.axis_index("tangent") == 0
    base = c * mine
    natural_order((w_0, w_1, w_2, w_3), w_oth)
    one = Halves(c, half, w_own, w_oth, 0)
    two = Halves(c, half, w_own, w_oth, 1)
    left, right = one.cols(0), one.cols(1)

    def layer_one(g):
        lo, hi = g * GROUP, (g + 1) * GROUP
        ts = (t_own[lo * per:hi * per, :], t_oth[pl.ds((base + lo) * per, GROUP * per), :])
        return one.apply_wide(ts, 1).reshape(GROUP, per, half)

    def finish_one(g, g1):
        lo, hi = g * GROUP, (g + 1) * GROUP
        c1_sc[lo:hi, :] = jnp.sum(g1 * g1, axis=1)
        return (g1 * slope1[lo:hi, None, right]).astype(BF16).reshape(GROUP * per, half)

    def layer_two(g, far):
        lo, hi = g * GROUP, (g + 1) * GROUP
        near = t2_own[lo:hi].reshape(GROUP * per, half)
        prod = None
        for j in (0, 1):
            if j == 0:
                g2 = g2_part[lo:hi] + mm_wide(far, two.block(1, 0)).reshape(GROUP, per, half)
            else:
                g2 = two.apply_wide((near, far), 1).reshape(GROUP, per, half)
            c2_sc[lo:hi, two.cols(j)] = jnp.sum(g2 * g2, axis=1)
            term = g2 * rs[j][lo:hi, None, :]
            prod = term if prod is None else prod + term
        grad_out[lo:hi, :] = jnp.sum(prod, axis=-1)

    vs = (vl_own[:walkers, :], vl_oth[:walkers, :])
    ls = [vl[pl.ds(walkers + base, mine), :] for vl in (vl_own, vl_oth)]
    pre = one.apply([jnp.concatenate([v, l], axis=0) for v, l in zip(vs, ls)], 1)
    lapin = [one.apply(ls, 0), pre[walkers:]]
    g1 = layer_one(0)
    hid = jnp.tanh(pre[:walkers] + one.vec(b1, 1))
    h_sc[:walkers, left] = aux[:walkers, :]
    h_sc[:walkers, right] = hid
    h1 = h_sc[pl.ds(base, mine), :]
    slope1 = 1.0 - h1 * h1
    value = [aux[:walkers, :].astype(BF16), hid.astype(BF16)]
    amp = None
    for j in (0, 1):
        hid = jnp.tanh(two.apply(value, j) + two.vec(b2, j))
        h_sc[walkers:, two.cols(j)] = hid
        term = two.vec(rd, j) * hid
        amp = term if amp is None else amp + term
    amp_out[...] = jnp.sum(amp[None], axis=-1)
    h2 = h_sc[pl.ds(walkers + base, mine), :]
    slope2 = 1.0 - h2 * h2
    rs = [two.vec(rd, j) * slope2[:, two.cols(j)] for j in (0, 1)]
    for g in range(mine // GROUP):
        far = finish_one(g, g1 if g == 0 else layer_one(g))
        layer_two(g, far)
    curv = [aux[walkers:, :], c1_sc[...]]
    laps = []
    for j in (0, 1):
        s1, h = slope1[:, one.cols(j)], h1[:, one.cols(j)]
        lap = jnp.where(first_z, s1 * lapin[j], 0.0) + (-2.0 * h * s1) * curv[j]
        high = lap.astype(BF16)
        laps.append(jnp.concatenate([high, (lap - high.astype(F32)).astype(BF16)], axis=0))
    lapin2 = [two.apply(laps, j) for j in (0, 1)]
    total = None
    for j in (0, 1):
        h = h2[:, two.cols(j)]
        term = rs[j] * (lapin2[j][:mine] + lapin2[j][mine:] + (-2.0 * h) * c2_sc[:, two.cols(j)])
        total = term if total is None else total + term
    gr = grad_out[...]
    row = jnp.sum(total[None], axis=-1) + jnp.sum((gr * gr)[None], axis=-1)
    pair = jnp.concatenate([row, row], axis=1)
    lane = lax.broadcasted_iota(jnp.int32, pair.shape, 1)
    pair = jnp.where((lane >= base) & (lane < base + mine), pair, 0.0)
    s_out[...] = jnp.zeros_like(s_out)
    s_out[:, :walkers] = jnp.broadcast_to(pair, (s_out.shape[0], walkers))


def join_kernel(sums, grad, g_oth, amp, amp_out, grad_out, kin_out):
    mine = grad.shape[0]
    walkers = amp.shape[1]
    c = lax.axis_index("feat")
    amp_out[...] = amp[...]
    grad_out[pl.ds(c * mine, mine), :] = grad[...]
    grad_out[pl.ds((1 - c) * mine, mine), :] = g_oth[...]
    kin_out[...] = -0.5 * sums[:, :walkers]


def in_hbm(x):
    return pltpu.with_memory_space_constraint(x, pltpu.HBM)


def per_device(value_in, tang_in, lap_in, w_first, b_first, w_second, b_second, readout):
    walkers, half = value_in.shape
    per = tang_in.shape[1]
    n_z, n_c = lax.axis_size("tangent"), lax.axis_size("feat")
    n_x, n_y = lax.axis_size("wx"), lax.axis_size("wy")
    mine = walkers // n_c
    peers = n_z * n_c
    rows = w_first.shape[0]
    swap = [(0, 1), (1, 0)]

    flat = tang_in.reshape(walkers * per, half)
    vm = pl.BlockSpec(memory_space=pltpu.VMEM)
    hbm = pl.BlockSpec(memory_space=pltpu.HBM)
    params = pltpu.CompilerParams(vmem_limit_bytes=24 * 1024 * 1024)
    sent = pl.pallas_call(
        prep_kernel,
        out_shape=jax.ShapeDtypeStruct((n_x * peers, 2, rows, half), BF16),
        in_specs=[hbm] * 2,
        out_specs=vm,
        scratch_shapes=[pltpu.VMEM((2, rows, n_c * half), BF16), pltpu.SemaphoreType.DMA((2,))],
        compiler_params=params,
        name="prep",
    )(in_hbm(w_first), in_hbm(w_second))
    t_oth = lax.ppermute(flat, "feat", swap)
    got = lax.all_to_all(sent, ("wx", "tangent", "feat"), 0, 0, tiled=True)
    block = pl.pallas_call(
        block_kernel,
        out_shape=jax.ShapeDtypeStruct((2 * n_x * peers * rows, half), BF16),
        in_specs=[vm],
        out_specs=vm,
        compiler_params=params,
        name="block",
    )(got)
    near, far = [block] * n_y, [None] * n_y
    for d in (2, 1, 3):
        near[d] = lax.ppermute(block, "wy", [(i, (i + d) % n_y) for i in range(n_y)])
    for d in (0, 2, 1, 3):
        far[d] = lax.ppermute(near[d], "feat", swap)

    width = 2 * half
    t_own, vl_own, vecs = pl.pallas_call(
        fetch_kernel,
        out_shape=(
            jax.ShapeDtypeStruct((mine * per, half), BF16),
            jax.ShapeDtypeStruct((2 * walkers, half), BF16),
            jax.ShapeDtypeStruct((3, 1, width), F32),
        ),
        in_specs=[hbm] * 6,
        out_specs=(vm, vm, vm),
        scratch_shapes=[pltpu.SemaphoreType.DMA((6,))],
        compiler_params=params,
        name="fetch",
    )(*(in_hbm(x) for x in (flat, value_in, lap_in, b_first[None], b_second[None], readout[None])))
    vl_oth = lax.ppermute(vl_own, "feat", swap)
    t2_own, g2_part, aux, w_own = pl.pallas_call(
        own_columns_kernel,
        out_shape=(
            jax.ShapeDtypeStruct((mine, per, half), BF16),
            jax.ShapeDtypeStruct((mine, per, half), F32),
            jax.ShapeDtypeStruct((walkers + mine, half), F32),
            jax.ShapeDtypeStruct((n_x, 2, n_y, peers * rows, half), BF16),
        ),
        in_specs=[vm] * 9,
        out_specs=(vm, vm, vm, vm),
        compiler_params=params,
        cost_estimate=pl.CostEstimate(flops=mine * per * width * width, bytes_accessed=1 << 22, transcendentals=0),
        name="own_columns",
    )(t_own, t_oth, vl_own, vl_oth, *near, vecs)
    amp, grad, part = pl.pallas_call(
        rest_kernel,
        out_shape=(
            jax.ShapeDtypeStruct((1, walkers), F32),
            jax.ShapeDtypeStruct((mine, per), F32),
            jax.ShapeDtypeStruct((peers, LANES), F32),
        ),
        in_specs=[vm] * 13,
        out_specs=(vm, vm, vm),
        scratch_shapes=[
            pltpu.VMEM((2 * walkers, width), F32),
            pltpu.VMEM((mine, half), F32),
            pltpu.VMEM((mine, width), F32),
            pltpu.VMEM((n_x, 2, n_y, peers * rows, half), BF16),
        ],
        compiler_params=params,
        cost_estimate=pl.CostEstimate(flops=3 * mine * per * width * width, bytes_accessed=1 << 22, transcendentals=0),
        name="rest",
    )(t_own, t_oth, t2_own, g2_part, aux, vl_own, vl_oth, w_own, *far, vecs)

    g_oth = lax.ppermute(grad, "feat", swap)
    sums = lax.all_to_all(part.reshape(peers, 1, LANES), ("tangent", "feat"), 0, 0, tiled=True)
    total = jnp.sum(sums, axis=0)
    amp, gradient, kinetic = pl.pallas_call(
        join_kernel,
        out_shape=(
            jax.ShapeDtypeStruct((1, walkers), F32),
            jax.ShapeDtypeStruct((walkers, per), F32),
            jax.ShapeDtypeStruct((1, walkers), F32),
        ),
        in_specs=[vm] * 4,
        out_specs=(vm, vm, vm),
        compiler_params=pltpu.CompilerParams(vmem_limit_bytes=2 * 1024 * 1024),
        name="join",
    )(total, grad, g_oth, amp)
    return amp.reshape(walkers), gradient, kinetic.reshape(walkers)


def solution(mesh):
    walker, tangent, feat = mesh.devices.shape
    side = math.isqrt(walker)
    mesh = jax.sharding.Mesh(mesh.devices.reshape(side, side, tangent, feat), ("wx", "wy", "tangent", "feat"))
    placed = (
        P(("wx", "wy"), "feat"),
        P(("wx", "wy"), "tangent", "feat"),
        P(("wx", "wy"), "feat"),
        P(("wx", "wy", "tangent", "feat"), None),
        P(),
        P(("wx", "wy", "tangent", "feat"), None),
        P(),
        P(),
    )

    return jax.shard_map(
        per_device,
        mesh=mesh,
        in_specs=placed,
        out_specs=(P(("wx", "wy")), P(("wx", "wy"), "tangent"), P(("wx", "wy"))),
        check_vma=False,
    )
```
